32 devices in a mesh: row: 4 (over x, core), col: 8 (over z, y).
Axes of the slice: x: 2, y: 2, z: 4, core: 2. Of those that a mesh axis runs over, the one named last changes fastest.
Arguments:
- inputs: bfloat16 [4096, 2048], P(('row', 'col')), may hold values from -6 to 6
- cotangent: bfloat16 [4096, 2048], P(('row', 'col')), may hold values from -12 to 12
- attn_gain: bfloat16 [2048], replicated, may hold values from 0.5 to 1.5
- mlp_gain: bfloat16 [2048], replicated, may hold values from 0.5 to 1.5
- attn_router: bfloat16 [2048, 4], replicated, may hold values from -0.09375 to 0.09375
- mlp_router: bfloat16 [2048, 4], replicated, may hold values from -0.09375 to 0.09375
- kv_weight: bfloat16 [4096, 2048], P(('row', 'col')), may hold values from -0.125 to 0.125
- query_weight: bfloat16 [4, 2048, 2048], P('row'), may hold values from -0.125 to 0.125
- output_weight: bfloat16 [4, 2048, 2048], P('row'), may hold values from -1 to 1
- expert_weight: bfloat16 [4, 5632, 3, 2048], P('row', 'col'), may hold values from -0.125 to 0.125
- attn_routes: int32 [4, 1024, 2], P(None, 'col'), may hold values from 0 to 3, all different within a row
- mlp_routes: int32 [4, 1024, 2], P(None, 'col'), may hold values from 0 to 3, all different within a row
- prefix_len: int32 [4, 8], P(None, 'col'), may hold values from 0 to 128
Outputs:
- output: bfloat16 [4096, 2048], P(('row', 'col'))
- input_grad: float32 [4096, 2048], P(('row', 'col'))
- attn_gain_grad: float32 [2048], replicated
- mlp_gain_grad: float32 [2048], replicated
- attn_router_grad: float32 [2048, 4], replicated
- mlp_router_grad: float32 [2048, 4], replicated
- kv_weight_grad: float32 [4096, 2048], P(('row', 'col'))
- query_weight_grad: float32 [4, 2048, 2048], P('row', 'col')
- out_weight_grad: float32 [4, 2048, 2048], P('row', 'col')
- expert_weight_grad: float32 [4, 5632, 3, 2048], P('row', 'col')
The draws below stay inside these ranges and needn't reach their ends.
All inputs are finite; a program needn't handle non-finite values.
Results may differ from the reference program's by a relative error of at most 0.02.
Values may be sent and summed in bfloat16 or wider, within the bound.
No kernel may reach another device: no remote copies, remote signals or barrier semaphores. Data moves between devices by JAX's collectives and lax.ppermute only.
A program may use at most 576 MiB of HBM per device.

```python
import jax
import jax.numpy as jnp
from jax import lax

D = 2048
FF = 5632
HEAD_DIM = 128
TOP = 2
TOK_DEV = 128
HD = 2048
EXPERTS = 4
TOKENS = 4096
N_ROW = 4
N_COL = 8


def draw_cotangent(key, part):
    rows = jnp.arange(TOKENS, dtype=jnp.float32)[:, None]
    ramp = 1.0 + 2.0 * rows / TOKENS
    base = jnp.clip(jax.random.normal(key, (TOKENS, D), jnp.float32), -4.0, 4.0)
    return (base * ramp).astype(jnp.bfloat16)


def touch_ends(entries, key, smallest, largest):
    longest = entries.shape.index(max(entries.shape))
    spots = []
    for shift in (0, 1):
        where = [jax.random.randint(jax.random.fold_in(key, axis), (), 0, length) for axis, length in enumerate(entries.shape)]
        where[longest] = (where[longest] + shift) % entries.shape[longest]
        spots.append(tuple(where))
    return entries.at[spots[0]].set(smallest).at[spots[1]].set(largest)


def level_of(rng, shape, cuts, smallest, high):
    gain, own = 1.0, jax.random.fold_in(rng, 6)
    for position, parts in cuts:
        steps = jnp.exp(jax.random.uniform(jax.random.fold_in(own, position), (parts,), jnp.float32, smallest / len(cuts), high / len(cuts)))
        gain = gain * jnp.repeat(steps, shape[position] // parts).reshape([-1 if axis == position else 1 for axis in range(len(shape))])
    return gain


def picks_of(key, rows, number_of, top, lift):
    sequence = jax.random.permutation(jax.random.fold_in(key, 1), number_of)
    pull = sequence
    for power in range(3):
        pull = pull * pull // number_of
    pull = pull * lift // number_of
    chance = jax.random.randint(jax.random.fold_in(key, 2), (rows, number_of), 0, 4096) + pull
    fixed_rows = jax.random.permutation(jax.random.fold_in(key, 3), rows)[jnp.arange(number_of) % rows]
    chance = jnp.where(jnp.arange(rows)[:, None] == fixed_rows[None, :], 1 << 14, chance)
    priority = chance * number_of + jnp.arange(number_of)
    return lax.top_k(priority.astype(jnp.int32), top)[1].astype(jnp.int32)


def centred(key, shape, deviation, bound, pieces=(), kind=jnp.bfloat16):
    level = level_of(key, shape, pieces, -0.22, 0.18) if pieces else 1.0
    values = jax.random.normal(key, shape, jnp.float32) * deviation * level
    return jnp.minimum(jnp.maximum(values, -bound), bound).astype(kind)


def setup_inputs(seed: int = 0) -> dict:
    key_of = jax.random.split(jax.random.key(seed), 14)
    inputs = centred(key_of[0], (TOKENS, D), 1.0, 6.0, ((0, 32),))
    cotangent = draw_cotangent(jax.random.fold_in(key_of[13], 71), 0)
    attn_gain = jnp.clip(1.0 + 0.1 * jax.random.normal(key_of[2], (D,), jnp.float32), 0.5, 1.5).astype(jnp.bfloat16)
    mlp_gain = jnp.clip(1.0 + 0.1 * jax.random.normal(key_of[3], (D,), jnp.float32), 0.5, 1.5).astype(jnp.bfloat16)
    attn_router = centred(key_of[4], (D, EXPERTS), (2 * D) ** -0.5, 0.09375)
    mlp_router = centred(key_of[5], (D, EXPERTS), (2 * D) ** -0.5, 0.09375)
    kv_weight = centred(key_of[6], (2 * HD, D), D ** -0.5, 0.125, ((0, 32),))
    query_weight = centred(key_of[7], (EXPERTS, D, HD), D ** -0.5, 0.125, ((0, 4),))
    output_weight = centred(key_of[8], (EXPERTS, HD, D), (HD * 2 // TOK_DEV) ** -0.5, 1.0, ((0, 4),))
    expert_weight = centred(key_of[9], (EXPERTS, FF, 3, D), D ** -0.5, 0.125, ((0, 4), (1, 8)))
    attn_routes = picks_of(key_of[10], N_ROW * (N_COL * TOK_DEV), EXPERTS, TOP, 4096).reshape((N_ROW, N_COL * TOK_DEV, TOP))
    mlp_routes = picks_of(key_of[11], N_ROW * (N_COL * TOK_DEV), EXPERTS, TOP, 4096).reshape((N_ROW, N_COL * TOK_DEV, TOP))
    prefix_len = touch_ends(jax.random.randint(key_of[12], (N_ROW, N_COL), 0, TOK_DEV + 1), jax.random.fold_in(key_of[12], 1), 0, TOK_DEV).astype(jnp.int32)
    return dict(inputs=inputs, cotangent=cotangent, attn_gain=attn_gain, mlp_gain=mlp_gain, attn_router=attn_router, mlp_router=mlp_router, kv_weight=kv_weight, query_weight=query_weight, output_weight=output_weight, expert_weight=expert_weight, attn_routes=attn_routes, mlp_routes=mlp_routes, prefix_len=prefix_len)


eps = 1e-06
theta = 10000.0
far_below = -1e+30
precise = lax.Precision.HIGHEST

@jax.custom_vjp
def low(v):
    return lax.optimization_barrier(v.astype(jnp.bfloat16)).astype(jnp.float32)

@jax.custom_vjp
def low_back(v):
    return v

def low_keep(v):
    return (low(v), None)

def low_pass(kept, grad):
    return (grad,)

def back_keep(v):
    return (v, None)

def back_low(kept, grad):
    return (low(grad),)
low.defvjp(low_keep, low_pass)
low_back.defvjp(back_keep, back_low)

def normalize(values, gain_vector):
    return values * lax.rsqrt(lax.optimization_barrier(jnp.mean(values * values, axis=-1, keepdims=True)) + eps) * gain_vector

def rotary(values, positions):
    half_dim = HEAD_DIM // 2
    frequency = theta ** (-jnp.arange(half_dim, dtype=jnp.float32) / half_dim)
    angles = positions.astype(jnp.float32)[..., None, None] * frequency
    cosine = jnp.cos(angles)
    sine_table = jnp.sin(angles)
    front_half = values[..., :half_dim]
    back_half = values[..., half_dim:]
    return jnp.concatenate([front_half * cosine - back_half * sine_table, front_half * sine_table + back_half * cosine], axis=-1)

def slot_places(routes, capacity, experts):
    flat_routes = routes.reshape(-1).astype(jnp.int32)
    onehot = (flat_routes[:, None] == jnp.arange(experts, dtype=jnp.int32)[None, :]).astype(jnp.int32)
    before = (jnp.cumsum(onehot, axis=0) - onehot).astype(jnp.int32)
    slot_rank = lax.optimization_barrier(jnp.sum(before * onehot, axis=1)).astype(jnp.int32)
    return jnp.where(slot_rank < capacity, flat_routes * capacity + slot_rank, experts * capacity).astype(jnp.int32)

def slot_positions(places, length, slot_count):
    anchor = jnp.repeat(jnp.arange(length, dtype=jnp.int32), TOP)
    return jnp.zeros((slot_count + 1,), jnp.int32).at[places].set(anchor)[:slot_count]

def pair_gates(logits, routes):
    chosen = jnp.take_along_axis(logits, routes, axis=1)
    highest = lax.optimization_barrier(jnp.max(chosen, axis=1, keepdims=True))
    weights = jnp.exp(chosen - highest)
    return weights / lax.optimization_barrier(jnp.sum(weights, axis=1, keepdims=True))

def dispatch(rows, places, slot_count):
    return jnp.zeros((slot_count + 1, rows.shape[1]), jnp.float32).at[places].add(jnp.repeat(rows, TOP, axis=0))[:slot_count]

def combine(returned, places):
    padded = jnp.concatenate([returned, jnp.zeros((1, returned.shape[1]), jnp.float32)], axis=0)
    return padded[places].reshape(-1, TOP, returned.shape[1])

def sequence_layer(weight_set, tokens, routes_attn, routes_mlp, prefix):
    attn_gain, mlp_gain, attn_router, mlp_router, kv_weight, query_weight, output_weight, expert_weight = weight_set
    experts = query_weight.shape[0]
    capacity = TOK_DEV * TOP // experts
    slot_count = experts * capacity
    head_count = HD // HEAD_DIM
    positions = jnp.arange(TOK_DEV, dtype=jnp.int32)
    normed = low(normalize(tokens, attn_gain))
    gates_attn = pair_gates(jnp.dot(normed, attn_router, precision=precise), routes_attn)
    projected = jnp.dot(normed, kv_weight.T, precision=precise)
    keys = low(rotary(low_back(projected[:, :HD]).reshape(TOK_DEV, head_count, HEAD_DIM), positions))
    values = low(low_back(projected[:, HD:])).reshape(TOK_DEV, head_count, HEAD_DIM)
    places_attn = slot_places(routes_attn, capacity, experts)
    where_from = slot_positions(places_attn, TOK_DEV, slot_count).reshape(experts, capacity)
    arrived = low_back(dispatch(normed, places_attn, slot_count)).reshape(experts, capacity, D)
    queries = jnp.einsum('ecd,edh->ech', arrived, query_weight, precision=precise)
    queries = low(rotary(low_back(queries).reshape(experts, capacity, head_count, HEAD_DIM), where_from))
    raw_scores = low_back(jnp.einsum('echd,lhd->ehcl', queries, keys, precision=precise) * HEAD_DIM ** (-0.5))
    allowed = (positions[None, None, :] <= where_from[:, :, None]) | (positions[None, None, :] < prefix)
    masked = jnp.where(allowed[:, None], raw_scores, far_below)
    row_peak = lax.optimization_barrier(jnp.max(masked, axis=-1, keepdims=True))
    exponent = jnp.exp(masked - row_peak)
    attention = low(exponent / lax.optimization_barrier(jnp.sum(exponent, axis=-1, keepdims=True)))
    attended = jnp.einsum('ehcl,lhd->echd', attention, values, precision=precise).reshape(experts, capacity, HD)
    attended = low(low_back(attended))
    answers = jnp.einsum('ech,ehd->ecd', attended, output_weight, precision=precise)
    answers = low(low_back(answers)).reshape(slot_count, D)
    mixed = tokens + lax.optimization_barrier(jnp.sum(gates_attn[:, :, None] * combine(answers, places_attn), axis=1))
    normed_mlp = low(normalize(mixed, mlp_gain))
    gates_mlp = pair_gates(jnp.dot(normed_mlp, mlp_router, precision=precise), routes_mlp)
    places_mlp = slot_places(routes_mlp, capacity, experts)
    arrived_mlp = low_back(dispatch(normed_mlp, places_mlp, slot_count)).reshape(experts, capacity, D)
    gate_pre = low_back(jnp.einsum('ecd,efd->ecf', arrived_mlp, expert_weight[:, :, 0, :], precision=precise))
    up_pre = low_back(jnp.einsum('ecd,efd->ecf', arrived_mlp, expert_weight[:, :, 1, :], precision=precise))
    hidden = low(gate_pre * jax.nn.sigmoid(gate_pre) * up_pre)
    down_out = jnp.einsum('ecf,efd->ecd', hidden, expert_weight[:, :, 2, :], precision=precise)
    down_out = low(low_back(down_out)).reshape(slot_count, D)
    return mixed + lax.optimization_barrier(jnp.sum(gates_mlp[:, :, None] * combine(down_out, places_mlp), axis=1))

def reference(inputs, cotangent, attn_gain, mlp_gain, attn_router, mlp_router, kv_weight, query_weight, output_weight, expert_weight, attn_routes, mlp_routes, prefix_len):
    seq_count = N_ROW * N_COL
    weights = (attn_gain.astype(jnp.float32), mlp_gain.astype(jnp.float32), attn_router.astype(jnp.float32), mlp_router.astype(jnp.float32), kv_weight.astype(jnp.float32), query_weight.astype(jnp.float32), output_weight.astype(jnp.float32), expert_weight.astype(jnp.float32))
    tokens = inputs.astype(jnp.float32).reshape(seq_count, TOK_DEV, D)
    routes_attn = attn_routes.reshape(seq_count, TOK_DEV, TOP)
    routes_mlp = mlp_routes.reshape(seq_count, TOK_DEV, TOP)
    prefixes = prefix_len.reshape(seq_count)

    def forward(token_rows, weight_set):

        def one_sequence(packed):
            return jax.checkpoint(sequence_layer)(weight_set, packed[0], packed[1], packed[2], packed[3])
        return lax.map(one_sequence, (token_rows, routes_attn, routes_mlp, prefixes))
    result, pullback = jax.vjp(forward, tokens, weights)
    token_grad, weight_grads = pullback(cotangent.astype(jnp.float32).reshape(seq_count, TOK_DEV, D))
    return (result.reshape(TOKENS, D).astype(jnp.bfloat16), token_grad.reshape(TOKENS, D), weight_grads[0], weight_grads[1], weight_grads[2], weight_grads[3], weight_grads[4], weight_grads[5], weight_grads[6], weight_grads[7])
```

```python
import functools

import jax
import jax.numpy as jnp
from jax import lax
from jax.experimental import pallas as pl
from jax.experimental.pallas import tpu as pltpu
from jax.sharding import PartitionSpec as P

HEAD_DIM = 128
TOP = 2
BOTH = ("row", "col")

eps = 1e-06
theta = 10000.0
far_below = -1e30
F32 = jnp.float32
LOW = jnp.bfloat16


def dot(left, right, left_dim, right_dim):
    return lax.dot_general(
        left, right, (((left_dim,), (right_dim,)), ((), ())), preferred_element_type=F32
    )


def rope_tables(length):
    half_dim = HEAD_DIM // 2
    frequency = theta ** (-jnp.arange(half_dim, dtype=F32) / half_dim)
    angles = jnp.arange(length, dtype=F32)[:, None] * frequency
    cosine, sine = jnp.cos(angles), jnp.sin(angles)
    return (
        jnp.concatenate([cosine, cosine], axis=1),
        jnp.concatenate([-sine, sine], axis=1),
    )


def swap_halves(values):
    return pltpu.roll(values, HEAD_DIM // 2, 1)


def probabilities(query, key, allowed, scale):
    scores = jnp.where(allowed, dot(query, key, 1, 1) * scale, far_below)
    exponent = jnp.exp(scores - jnp.max(scores, axis=1, keepdims=True))
    return exponent / jnp.sum(exponent, axis=1, keepdims=True)


def allowed_keys(prefix, length):
    query_at = lax.broadcasted_iota(jnp.int32, (length, length), 0)
    key_at = lax.broadcasted_iota(jnp.int32, (length, length), 1)
    return (key_at <= query_at) | (key_at < prefix)


def attend_kernel(
    seqs, length, width, scale,
    prefix_ref, tok_ref, gain_ref, wkv_ref, wq_ref, cos_ref, sin_ref, sel_ref,
    normed_ref, q_ref, k_ref, v_ref, att_ref, slot_ref,
):
    first = pl.program_id(0) * seqs
    tokens = tok_ref[...].astype(F32)
    inverse = lax.rsqrt(jnp.mean(tokens * tokens, axis=1, keepdims=True) + eps)
    normed = (tokens * inverse * gain_ref[...]).astype(LOW)
    normed_ref[...] = normed
    kv = dot(normed, wkv_ref[...], 1, 1)
    qs = dot(normed, wq_ref[...], 1, 0)
    cosine, sine = cos_ref[...], sin_ref[...]
    v_ref[...] = kv[:, width:].astype(LOW)
    for s in range(seqs):
        rows = slice(s * length, (s + 1) * length)
        allowed = allowed_keys(prefix_ref[first + s], length)
        for h in range(width // HEAD_DIM):
            cols = slice(h * HEAD_DIM, (h + 1) * HEAD_DIM)
            key = kv[rows, cols]
            key = (key * cosine + swap_halves(key) * sine).astype(LOW)
            query = qs[rows, cols]
            query = (query * cosine + swap_halves(query) * sine).astype(LOW)
            k_ref[rows, cols] = key
            q_ref[rows, cols] = query
            probs = probabilities(query, key, allowed, scale).astype(LOW)
            att_ref[rows, cols] = dot(probs, v_ref[rows, cols], 1, 0).astype(LOW)
        slot_ref[s, 0] = dot(sel_ref[s], att_ref[rows, :], 1, 0).astype(LOW)


def attend_back_kernel(
    seqs, length, width, scale,
    prefix_ref, mg_ref, wo_ref, gate_ref, q_ref, k_ref, v_ref, att_ref, cos_ref, sin_ref, sel_ref,
    dq_ref, dkv_ref, attg_ref, slot_ref,
):
    first = pl.program_id(0) * seqs
    raw = dot(mg_ref[...], wo_ref[...], 1, 1)
    cosine, sine = cos_ref[...], sin_ref[...]
    for s in range(seqs):
        rows = slice(s * length, (s + 1) * length)
        allowed = allowed_keys(prefix_ref[first + s], length)
        gate = jnp.broadcast_to(gate_ref[s], (HEAD_DIM, length)).T
        for h in range(width // HEAD_DIM):
            cols = slice(h * HEAD_DIM, (h + 1) * HEAD_DIM)
            vcols = slice(width + h * HEAD_DIM, width + (h + 1) * HEAD_DIM)
            query, key, value = q_ref[rows, cols], k_ref[rows, cols], v_ref[rows, cols]
            probs = probabilities(query, key, allowed, scale)
            att_grad = (raw[rows, cols] * gate).astype(LOW)
            attg_ref[rows, cols] = (att_ref[rows, cols].astype(F32) * gate).astype(LOW)
            prob_grad = dot(att_grad, value, 1, 1)
            delta = jnp.sum(probs * prob_grad, axis=1, keepdims=True)
            score_grad = (probs * (prob_grad - delta)).astype(LOW)
            dq = dot(score_grad, key, 1, 0) * scale
            dq_ref[rows, cols] = (dq * cosine - swap_halves(dq) * sine).astype(LOW)
            dk = dot(score_grad, query, 0, 0) * scale
            dkv_ref[rows, cols] = (dk * cosine - swap_halves(dk) * sine).astype(LOW)
            dkv_ref[rows, vcols] = dot(probs.astype(LOW), att_grad, 0, 0).astype(LOW)
        slot_ref[s, 0] = dot(sel_ref[s], dq_ref[rows, :], 1, 0).astype(LOW)


def expert_kernel(
    seqs, length, capacity,
    nm_ref, up_ref, sel_ref, gate_ref, wg_ref, wu_ref, wd_ref,
    x_ref, u_ref, gg_ref, ug_ref, hg_ref, dx_ref, down_ref, part_ref,
):
    gates = []
    for s in range(seqs):
        rows = slice(s * length, (s + 1) * length)
        slots = slice(s * capacity, (s + 1) * capacity)
        sel = sel_ref[s]
        x_ref[slots, :] = dot(sel, nm_ref[rows, :], 1, 0).astype(LOW)
        u_ref[slots, :] = dot(sel, up_ref[rows, :], 1, 0).astype(LOW)
        gates.append(jnp.sum(sel.astype(F32) * gate_ref[s], axis=1, keepdims=True))
    gate = jnp.concatenate(gates, axis=0)
    x, u = x_ref[...], u_ref[...]
    pre = dot(x, wg_ref[...], 1, 1)
    up = dot(x, wu_ref[...], 1, 1)
    sig = 1.0 / (1.0 + jnp.exp(-pre))
    act = pre * sig
    hidden = (act * up).astype(LOW)
    raw = dot(u, wd_ref[...], 1, 1)
    wide = hidden.astype(F32)
    part = jnp.sum(wide * raw, axis=1, keepdims=True)
    part_ref[...] = jnp.broadcast_to(part, part_ref.shape)
    hg_ref[...] = (wide * gate).astype(LOW)
    grad = raw * gate
    gate_grad = (grad * up * sig * (1.0 + pre * (1.0 - sig))).astype(LOW)
    up_grad = (grad * act).astype(LOW)
    gg_ref[...] = gate_grad
    ug_ref[...] = up_grad
    dx = dot(gate_grad, wg_ref[...], 1, 0) + dot(up_grad, wu_ref[...], 1, 0)
    dx = dx.astype(LOW)
    down = dot(hidden, wd_ref[...], 1, 0).astype(LOW)
    for s in range(seqs):
        slots = slice(s * capacity, (s + 1) * capacity)
        dx_ref[s, 0] = dx[slots]
        down_ref[s, 0] = down[slots]


def const_spec(shape):
    return pl.BlockSpec(shape, lambda g, *_: (0,) * len(shape), pipeline_mode=pl.Buffered(1))


def row_spec(rows, cols):
    return pl.BlockSpec((rows, cols), lambda g, *_: (g, 0))


def lead_spec(count, *rest):
    return pl.BlockSpec((count,) + rest, lambda g, *_: (g,) + (0,) * len(rest))


def slot_spec(seqs, per_row, capacity, cols):
    return pl.BlockSpec(
        (seqs, 1, capacity, cols), lambda g, *_: (g % per_row, g // per_row, 0, 0)
    )


def trade(buffer, axis="row"):
    return lax.all_to_all(buffer, axis, split_axis=0, concat_axis=0, tiled=True)


def spread(values, axis, size):
    return trade(jnp.broadcast_to(values[None], (size,) + values.shape), axis)


def after(values, *others):
    return lax.optimization_barrier((values,) + others)[0]


def small_total(values, devices):
    pieces = trade(values.reshape(devices, -1), BOTH)
    piece = jnp.sum(pieces, axis=0)
    return spread(piece, BOTH, devices).reshape(-1)


def ranks(hit):
    length = hit.shape[-1]
    earlier = jnp.arange(length)[:, None] < jnp.arange(length)[None, :]
    flat = hit.reshape(-1, length).astype(LOW)
    return dot(flat, earlier.astype(LOW), 1, 0).reshape(hit.shape).astype(jnp.int32)


def selection(hit, capacity):
    slot = jnp.arange(capacity, dtype=jnp.int32)[:, None]
    return hit[..., None, :] & (ranks(hit)[..., None, :] == slot)


def routed_gates(normed_low, router, chosen):
    logits = jnp.dot(normed_low, router, preferred_element_type=F32)
    highest = jnp.max(jnp.where(chosen, logits, -jnp.inf), axis=1, keepdims=True)
    weights = jnp.where(chosen, jnp.exp(jnp.minimum(logits - highest, 0.0)), 0.0)
    return weights / jnp.sum(weights, axis=1, keepdims=True)


def outer_sum(weights, table):
    total = weights[:, 0:1] * table[:, 0][None, :]
    for e in range(1, weights.shape[1]):
        total = total + weights[:, e : e + 1] * table[:, e][None, :]
    return total


def router_term(normed_low, logit_grad):
    return jnp.dot(normed_low.astype(F32).T, logit_grad, precision=lax.Precision.HIGHEST)


def scattered(sel, rows):
    return jnp.stack([dot(sel[e], rows[e], 0, 0) for e in range(sel.shape[0])])


def local(
    inputs, cotangent, attn_gain, mlp_gain, attn_router, mlp_router, kv_weight, query_weight,
    output_weight, expert_weight, attn_routes, mlp_routes, prefix_len,
):
    length, model = inputs.shape
    n_row, n_col = lax.axis_size("row"), lax.axis_size("col")
    devices = n_row * n_col
    experts = n_row
    total = devices * length
    capacity = length * TOP // experts
    slots = n_row * capacity
    head_width = query_weight.shape[2]
    width = head_width // n_col
    hidden = expert_weight.shape[1]
    scale = HEAD_DIM ** (-0.5)
    own_row, own_col = lax.axis_index("row"), lax.axis_index("col")
    seqs = 4 if n_col % 4 == 0 else 1
    per_row = n_col // seqs
    steps = devices // seqs

    packed = jnp.concatenate(
        [attn_routes.reshape(-1), mlp_routes.reshape(-1), prefix_len.reshape(-1)]
    )
    packed = spread(packed, "col", n_col)
    span = n_row * length * TOP
    routes_a = packed[:, :span].reshape(n_col, n_row, length, TOP)
    routes_m = packed[:, span : 2 * span].reshape(n_col, n_row, length, TOP)
    prefixes = packed[:, 2 * span :].T.reshape(-1)
    routes_a = routes_a.transpose(1, 0, 2, 3).reshape(devices, length, TOP)
    routes_m = routes_m.transpose(1, 0, 2, 3).reshape(devices, length, TOP)
    sel_a = selection(jnp.any(routes_a == own_row, axis=-1), capacity).astype(LOW)
    sel_m = selection(jnp.any(routes_m == own_row, axis=-1), capacity).astype(LOW)

    def own_side(routes):
        own = lax.dynamic_index_in_dim(routes, own_row, 0, keepdims=False)
        each = jnp.arange(experts, dtype=jnp.int32)
        chosen = jnp.any(own[:, :, None] == each[None, None, :], axis=1)
        sel = selection(chosen.T, capacity)
        kept = jnp.any(sel, axis=1).T
        return chosen, sel, kept

    chosen_a, own_sel_a, kept_a = own_side(attn_routes)
    chosen_m, own_sel_m, kept_m = own_side(mlp_routes)
    own_sel_a_low, own_sel_m_low = own_sel_a.astype(LOW), own_sel_m.astype(LOW)

    half = n_row // 2
    route_kv = []
    for d in range(devices):
        at = d % (devices // 2)
        route_kv.append((d, (at % half + half * (2 * d // devices)) * n_col + at // half))
    back_kv = [(b, a) for a, b in route_kv]
    kv_block = lax.ppermute(kv_weight, BOTH, route_kv)
    kv_rows = spread(kv_block, "row", n_row).reshape(2 * width, model)
    wq = lax.dynamic_slice_in_dim(query_weight[0], own_col * width, width, 1)
    wo = lax.dynamic_slice_in_dim(output_weight[0], own_col * width, width, 0)

    tok_all = lax.all_gather(inputs, BOTH, axis=0, tiled=True)
    up_all = lax.all_gather(after(cotangent, tok_all), BOTH, axis=0, tiled=True)

    cosine, sine = rope_tables(length)
    gain_attn, gain_mlp = attn_gain.astype(F32), mlp_gain.astype(F32)
    rows = seqs * length
    token_out = jax.ShapeDtypeStruct((total, width), LOW)
    slot_out = jax.ShapeDtypeStruct((n_col, n_row, capacity, width), LOW)
    params = pltpu.CompilerParams(vmem_limit_bytes=60 * 2**20)
    normed_all, q_all, k_all, v_all, att_all, att_slots = pl.pallas_call(
        functools.partial(attend_kernel, seqs, length, width, scale),
        grid_spec=pltpu.PrefetchScalarGridSpec(
            num_scalar_prefetch=1,
            grid=(steps,),
            in_specs=[
                row_spec(rows, model),
                const_spec((1, model)),
                const_spec((2 * width, model)),
                const_spec((model, width)),
                const_spec((length, HEAD_DIM)),
                const_spec((length, HEAD_DIM)),
                lead_spec(seqs, capacity, length),
            ],
            out_specs=[row_spec(rows, model)]
            + [row_spec(rows, width)] * 4
            + [slot_spec(seqs, per_row, capacity, width)],
        ),
        out_shape=[jax.ShapeDtypeStruct((total, model), LOW)] + [token_out] * 4 + [slot_out],
        compiler_params=params,
        name="attend",
    )(prefixes, tok_all, gain_attn[None], kv_rows, wq, cosine, sine, sel_a)

    attended = trade(att_slots.reshape(n_col, slots, width), "col")
    attended = attended.transpose(1, 0, 2).reshape(slots, head_width)
    answers = dot(attended, output_weight[0], 1, 0).astype(LOW)
    returned = trade(answers.reshape(n_row, capacity, model))
    tokens = inputs.astype(F32)
    inverse_a = lax.rsqrt(jnp.mean(tokens * tokens, axis=-1, keepdims=True) + eps)
    normed_low = (tokens * inverse_a * gain_attn).astype(LOW)
    gates_a = routed_gates(normed_low, attn_router, chosen_a)
    kept_gates_a = jnp.where(kept_a, gates_a, 0.0)
    pairs_a = scattered(own_sel_a_low, returned)
    mixed = tokens + jnp.sum(kept_gates_a.T[:, :, None] * pairs_a, axis=0)
    inverse_m = lax.rsqrt(jnp.mean(mixed * mixed, axis=-1, keepdims=True) + eps)
    normed_m = (mixed * inverse_m * gain_mlp).astype(LOW)
    nm_all = lax.all_gather(after(normed_m, up_all), BOTH, axis=0, tiled=True)
    gates_m = routed_gates(normed_m, mlp_router, chosen_m)
    kept_gates_m = jnp.where(kept_m, gates_m, 0.0)
    gate_table = lax.all_gather(
        jnp.concatenate([kept_gates_a, kept_gates_m], axis=1).T, BOTH, axis=0
    )
    gate_a_all = lax.dynamic_index_in_dim(gate_table, own_row, 1)
    gate_m_all = lax.dynamic_index_in_dim(gate_table, experts + own_row, 1)

    block = expert_weight[0]
    slot_rows = seqs * capacity
    wide_slots = jax.ShapeDtypeStruct((devices * capacity, model), LOW)
    hidden_slots = jax.ShapeDtypeStruct((devices * capacity, hidden), LOW)
    grouped = jax.ShapeDtypeStruct((n_col, n_row, capacity, model), LOW)
    x, u, gg, ug, hg, dx, down, part = pl.pallas_call(
        functools.partial(expert_kernel, seqs, length, capacity),
        grid_spec=pltpu.PrefetchScalarGridSpec(
            num_scalar_prefetch=0,
            grid=(steps,),
            in_specs=[
                row_spec(rows, model),
                row_spec(rows, model),
                lead_spec(seqs, capacity, length),
                lead_spec(seqs, 1, length),
                const_spec((hidden, model)),
                const_spec((hidden, model)),
                const_spec((hidden, model)),
            ],
            out_specs=[row_spec(slot_rows, model)] * 2
            + [row_spec(slot_rows, hidden)] * 3
            + [slot_spec(seqs, per_row, capacity, model)] * 2
            + [row_spec(slot_rows, 128)],
        ),
        out_shape=[wide_slots] * 2
        + [hidden_slots] * 3
        + [grouped] * 2
        + [jax.ShapeDtypeStruct((devices * capacity, 128), F32)],
        compiler_params=params,
        name="experts",
    )(nm_all, up_all, sel_m, gate_m_all, block[:, 0], block[:, 1], block[:, 2])
    dx_sum = lax.psum_scatter(
        dx.reshape(-1, model), "col", scatter_dimension=0, tiled=True
    )
    back_m = trade(dx_sum.reshape(n_row, capacity, model))
    parts = trade(part[:, 0].reshape(devices, capacity), BOTH)
    parts = jnp.sum(parts.reshape(experts, n_col, capacity), axis=1)
    gate_grad_m = jnp.sum(jnp.where(own_sel_m, parts[:, :, None], 0.0), axis=1).T

    def logit_grads(gates, grads):
        return gates * (grads - jnp.sum(gates * grads, axis=1, keepdims=True))

    logit_m = logit_grads(gates_m, gate_grad_m)
    normed_m_grad = jnp.sum(scattered(own_sel_m_low, back_m), axis=0)
    normed_m_grad = normed_m_grad + outer_sum(logit_m, mlp_router.astype(F32))
    upstream = cotangent.astype(F32)
    scaled = normed_m_grad * gain_mlp
    inner = jnp.mean(scaled * mixed, axis=-1, keepdims=True)
    mixed_grad = upstream + inverse_m * scaled - mixed * inverse_m * inverse_m * inverse_m * inner
    mg_all = lax.all_gather(mixed_grad.astype(LOW), BOTH, axis=0, tiled=True)

    down_sum = lax.psum_scatter(
        after(down.reshape(-1, model), mg_all), "col", scatter_dimension=0, tiled=True
    )
    back_down = trade(down_sum.reshape(n_row, capacity, model))
    pairs_m = scattered(own_sel_m_low, back_down)
    output = (mixed + jnp.sum(kept_gates_m.T[:, :, None] * pairs_m, axis=0)).astype(LOW)
    expert_grad = jnp.stack([dot(gg, x, 0, 0), dot(ug, x, 0, 0), dot(hg, u, 0, 0)], axis=1)
    mlp_gain_term = jnp.sum(normed_m_grad * mixed * inverse_m, axis=0)
    gate_grad_a = jnp.sum(pairs_a * mixed_grad[None], axis=-1).T
    logit_a = logit_grads(gates_a, gate_grad_a)
    early = small_total(
        jnp.concatenate(
            [
                mlp_gain_term,
                router_term(normed_m, logit_m).reshape(-1),
                router_term(normed_low, logit_a).reshape(-1),
            ]
        ),
        devices,
    )

    dq_all, dkv, attg, dq_slots = pl.pallas_call(
        functools.partial(attend_back_kernel, seqs, length, width, scale),
        grid_spec=pltpu.PrefetchScalarGridSpec(
            num_scalar_prefetch=1,
            grid=(steps,),
            in_specs=[
                row_spec(rows, model),
                const_spec((width, model)),
                lead_spec(seqs, 1, length),
            ]
            + [row_spec(rows, width)] * 4
            + [
                const_spec((length, HEAD_DIM)),
                const_spec((length, HEAD_DIM)),
                lead_spec(seqs, capacity, length),
            ],
            out_specs=[
                row_spec(rows, width),
                row_spec(rows, 2 * width),
                row_spec(rows, width),
                slot_spec(seqs, per_row, capacity, width),
            ],
        ),
        out_shape=[
            token_out,
            jax.ShapeDtypeStruct((total, 2 * width), LOW),
            token_out,
            slot_out,
        ],
        compiler_params=params,
        name="attend_back",
    )(prefixes, mg_all, wo, gate_a_all, q_all, k_all, v_all, att_all, cosine, sine, sel_a)

    piece = 2 * width // n_row
    dkv = trade(dkv.reshape(total, n_row, piece).transpose(1, 0, 2))
    projected_grad = jnp.sum(dkv.astype(F32), axis=0).astype(LOW)
    dq_own = trade(dq_slots.reshape(n_col, slots, width), "col")
    dq_own = dq_own.transpose(1, 0, 2).reshape(slots, head_width)
    arrived_grad = dot(dq_own, query_weight[0], 1, 1).astype(LOW)
    back_a = trade(arrived_grad.reshape(n_row, capacity, model))
    own_grad = trade(projected_grad.reshape(devices, length, piece), BOTH)
    own_grad = own_grad.transpose(1, 0, 2).reshape(length, 2 * head_width)
    kv_whole = lax.all_gather(after(kv_block, up_all), BOTH, axis=0, tiled=True)
    normed_grad = jnp.sum(scattered(own_sel_a_low, back_a), axis=0)
    normed_grad = normed_grad + dot(own_grad, kv_whole, 1, 0)
    normed_grad = normed_grad + outer_sum(logit_a, attn_router.astype(F32))
    scaled_a = normed_grad * gain_attn
    inner_a = jnp.mean(scaled_a * tokens, axis=-1, keepdims=True)
    input_grad = (
        mixed_grad + inverse_a * scaled_a - tokens * inverse_a * inverse_a * inverse_a * inner_a
    )
    attn_gain_term = jnp.sum(normed_grad * tokens * inverse_a, axis=0)
    attn_gain_grad = jnp.sum(lax.all_gather(attn_gain_term, BOTH, axis=0), axis=0)

    kv_grad = lax.ppermute(dot(projected_grad, normed_all, 0, 0), BOTH, back_kv)
    out_grad = dot(attg, mg_all, 0, 0)
    query_grad = trade(
        dot(normed_all, dq_all, 0, 0).astype(LOW).reshape(n_col, model // n_col, width), "col"
    )
    query_grad = query_grad.transpose(1, 0, 2).reshape(model // n_col, head_width).astype(F32)
    router_size = model * experts
    return (
        output,
        input_grad,
        attn_gain_grad,
        early[:model],
        early[model + router_size :].reshape(model, experts),
        early[model : model + router_size].reshape(model, experts),
        kv_grad,
        query_grad[None],
        out_grad[None],
        expert_grad[None],
    )


def solution(mesh):
    in_specs = (
        P(("row", "col"), None),
        P(("row", "col"), None),
        P(),
        P(),
        P(),
        P(),
        P(("row", "col"), None),
        P("row", None, None),
        P("row", None, None),
        P("row", "col", None, None),
        P(None, "col", None),
        P(None, "col", None),
        P(None, "col"),
    )
    out_specs = (
        P(("row", "col"), None),
        P(("row", "col"), None),
        P(),
        P(),
        P(),
        P(),
        P(("row", "col"), None),
        P("row", "col", None),
        P("row", "col", None),
        P("row", "col", None, None),
    )
    return jax.shard_map(local, mesh=mesh, in_specs=in_specs, out_specs=out_specs, check_vma=False)
```
